256 devices in a mesh: corpus: 64 (over y, z, x_hi), vocab: 4 (over x_lo, core).
Axes of the slice: x: 4 (x_hi: 2, x_lo: 2; x = x_hi * 2 + x_lo), y: 4, z: 8, core: 2. Of those that a mesh axis runs over, the one named last changes fastest.
Arguments:
- eval_tiles: bfloat16 [64, 12, 128, 512], P('corpus', 'vocab'), may hold values from 0.019897461 to 2
- eval_tile_list: int32 [64, 12], P(None, 'vocab'), may hold values from 0 to 128, as said below
- corpus_tiles: bfloat16 [256, 12, 128, 512], P('corpus', 'vocab'), may hold values from 0.019897461 to 2
- corpus_tile_list: int32 [256, 12], P('corpus', 'vocab'), may hold values from 0 to 128, as said below
- pair_eval_block: int32 [6144], P('corpus'), may hold values from 0 to 63
- pair_corpus_block: int32 [6144], P('corpus'), may hold values from 0 to 3
- pair_count: int32 [64], P('corpus'), may hold values from 12 to 96, as said below
- eval_norm: float32 [8192], replicated, may hold values from 8 to 32
- corpus_norm: float32 [32768], P('corpus'), may hold values from 8 to 32
Outputs:
- cosine_tiles: float32 [6144, 128, 128], P(('corpus', 'vocab'))
The draws below stay inside these ranges and needn't reach their ends.
Inputs may be any that keep to these rules, and one draw needn't show every extreme that they name: `eval_tile_list`: value 128 marks an empty slot; other ids of one row block in one slice are distinct. Slot 0 of a block and slice is never empty. `corpus_tile_list`: value 128 marks an empty slot; other ids of one row block in one slice are distinct. Slot 0 of a block and slice is never empty. Shard c's live pair slots are its first pair_count[c] slots. Some shard is full.
All inputs are finite; a program needn't handle non-finite values.
Results may differ from the reference program's by a relative error of at most 0.0003.
Values may be sent and summed in bfloat16 or wider, within the bound.
A program may use at most 128 MiB of HBM per device.

```python
import math
import jax
import jax.numpy as jnp
from jax import lax

TILE_ROWS = 128
TILE_TERMS = 512
SLOTS = 3
DB_DEV = 4
P_DEV = 96
SLICES = 4
SHARDS = 64
TILES_SLICE = 128
EB = 64
DB = 256
EVALS = 8192
DOCS = 32768
PAIRS = 6144


def tile_list(key, blocks):
    columns = SLICES * SLOTS
    column = jnp.arange(columns, dtype=jnp.int32)
    slice_of = column // SLOTS
    slot_of = column % SLOTS
    first_key, rest_key, vacant_key = jax.random.split(key, 3)
    frequent = jax.random.randint(first_key, (blocks, columns), 0, 3)
    rare_tiles = 3 + (slot_of - 1) * 2 + jax.random.randint(rest_key, (blocks, columns), 0, 2)
    chosen = jnp.where(slot_of == 0, frequent, rare_tiles)
    vacant = (jax.random.randint(vacant_key, (blocks, columns), 0, 2 * SLICES) < slice_of) & (slot_of > 0)
    block_row = jnp.arange(blocks, dtype=jnp.int32)[:, None]
    forced_vacant = (block_row == 0) & (slice_of == SLICES - 1) & (slot_of == 1)
    chosen = jnp.where(vacant | forced_vacant, TILES_SLICE, chosen)
    chosen = jnp.where((block_row == 0) & (column == 0), 0, chosen)
    return chosen.astype(jnp.int32)


def draw_eval_tile_list(key, part):
    return tile_list(jax.random.fold_in(key, 11), EB)


def draw_corpus_tile_list(key, part):
    return tile_list(jax.random.fold_in(key, 23), DB)


def draw_pair_count(key, part):
    light_key, heavy_key = jax.random.split(jax.random.fold_in(key, 37))
    lighter = jax.random.randint(light_key, (SHARDS,), P_DEV // 8, P_DEV // 2 + 1)
    busiest = jax.random.randint(heavy_key, (), 0, SHARDS)
    return jnp.where(jnp.arange(SHARDS) == busiest, P_DEV, lighter).astype(jnp.int32)


def plant(entries, rng, low, top_value):
    longest = entries.shape.index(max(entries.shape))
    spots = []
    for shift in (0, 1):
        where = [jax.random.randint(jax.random.fold_in(rng, axis), (), 0, length) for axis, length in enumerate(entries.shape)]
        where[longest] = (where[longest] + shift) % entries.shape[longest]
        spots.append(tuple(where))
    return entries.at[spots[0]].set(low).at[spots[1]].set(top_value)


def steps_of(rng, dims, pieces, smallest, largest):
    factor_of, own = 1.0, jax.random.fold_in(rng, 6)
    for axis_at, blocks in pieces:
        draws = jnp.exp(jax.random.uniform(jax.random.fold_in(own, axis_at), (blocks,), jnp.float32, smallest / len(pieces), largest / len(pieces)))
        factor_of = factor_of * jnp.repeat(draws, dims[axis_at] // blocks).reshape([-1 if axis == axis_at else 1 for axis in range(len(dims))])
    return factor_of


def setup_inputs(seed: int = 0) -> dict:
    arg_keys = jax.random.split(jax.random.key(seed), 10)
    eval_tiles = jnp.clip(jnp.exp(math.log(2.0) - 4.61031033 * jax.random.uniform(arg_keys[0], (EB, SLICES * SLOTS, TILE_ROWS, TILE_TERMS), jnp.float32) ** steps_of(arg_keys[0], (EB, SLICES * SLOTS, TILE_ROWS, TILE_TERMS), ((0, 64), (1, 4)), -0.2, 0.2)), 0.019897461, 2.0).astype(jnp.bfloat16)
    eval_tile_list = draw_eval_tile_list(jax.random.fold_in(arg_keys[9], 71), 0)
    corpus_tiles = jnp.clip(jnp.exp(math.log(2.0) - 4.61031033 * jax.random.uniform(arg_keys[2], (DB, SLICES * SLOTS, TILE_ROWS, TILE_TERMS), jnp.float32) ** steps_of(arg_keys[2], (DB, SLICES * SLOTS, TILE_ROWS, TILE_TERMS), ((0, 64), (1, 4)), -0.2, 0.2)), 0.019897461, 2.0).astype(jnp.bfloat16)
    corpus_tile_list = draw_corpus_tile_list(jax.random.fold_in(arg_keys[9], 71), 0)
    pair_eval_block = plant(jax.random.randint(arg_keys[4], (PAIRS,), 0, EB), jax.random.fold_in(arg_keys[4], 1), 0, EB - 1).astype(jnp.int32)
    pair_corpus_block = plant(jax.random.randint(arg_keys[5], (PAIRS,), 0, DB_DEV), jax.random.fold_in(arg_keys[5], 1), 0, DB_DEV - 1).astype(jnp.int32)
    pair_count = draw_pair_count(jax.random.fold_in(arg_keys[9], 71), 0)
    eval_norm = jnp.clip(jnp.exp(jax.random.uniform(arg_keys[7], (EVALS,), jnp.float32, math.log(8.0), math.log(32.0))), 8.0, 32.0)
    corpus_norm = jnp.clip(jnp.exp(math.log(32.0) - 1.3862944 * jax.random.uniform(arg_keys[8], (DOCS,), jnp.float32) ** steps_of(arg_keys[8], (DOCS,), ((0, 64),), -0.2, 0.2)), 8.0, 32.0)
    return {"eval_tiles": eval_tiles, "eval_tile_list": eval_tile_list, "corpus_tiles": corpus_tiles, "corpus_tile_list": corpus_tile_list, "pair_eval_block": pair_eval_block, "pair_corpus_block": pair_corpus_block, "pair_count": pair_count, "eval_norm": eval_norm, "corpus_norm": corpus_norm}


def reference(eval_tiles, eval_tile_list, corpus_tiles, corpus_tile_list, pair_eval_block, pair_corpus_block, pair_count, eval_norm, corpus_norm):
    column = jnp.arange(SLICES * SLOTS, dtype=jnp.int32)
    same_slice = (column[:, None] // SLOTS) == (column[None, :] // SLOTS)
    eval_scale_all = eval_norm.reshape(EB, TILE_ROWS)
    corpus_scale_all = corpus_norm.reshape(DB, TILE_ROWS)

    def one_pair(pair):
        shard_index = pair // P_DEV
        eval_block = pair_eval_block[pair]
        corpus_block = shard_index * DB_DEV + pair_corpus_block[pair]
        eval_list = eval_tile_list[eval_block]
        corpus_list = corpus_tile_list[corpus_block]
        matched = same_slice & (eval_list[:, None] == corpus_list[None, :]) & (eval_list[:, None] < TILES_SLICE)
        eval_part = eval_tiles[eval_block].astype(jnp.float32)
        corpus_part = corpus_tiles[corpus_block].astype(jnp.float32)
        aligned = jnp.einsum("ij,jrt->irt", matched.astype(jnp.float32), corpus_part, precision=lax.Precision.HIGHEST)
        products = jnp.einsum("irt,ist->rs", eval_part, aligned, precision=lax.Precision.HIGHEST)
        cosine = products / (eval_scale_all[eval_block][:, None] * corpus_scale_all[corpus_block][None, :])
        alive_pair = (pair % P_DEV) < pair_count[shard_index]
        return jnp.where(alive_pair, cosine, jnp.zeros_like(cosine))

    batches = jnp.arange(PAIRS, dtype=jnp.int32).reshape(PAIRS // 8, 8)
    result = lax.map(jax.vmap(one_pair), batches)
    return result.reshape(PAIRS, TILE_ROWS, TILE_ROWS)
```

```python
import functools
import heapq

import jax
import jax.numpy as jnp
from jax import lax
from jax.experimental import pallas as pl
from jax.experimental.pallas import tpu as pltpu
from jax.sharding import PartitionSpec as P

MESH = pl.DeviceIdType.MESH
VOCAB = 262144
NZ = 8
CHUNK = 6


def place(ny):
    c = lax.axis_index("corpus")
    v = lax.axis_index("vocab")
    h = lax.rem(c, 2)
    t = lax.div(c, 2)
    return lax.div(t, NZ), lax.rem(t, NZ), h, lax.div(v, 2), lax.rem(v, 2)


def device(y, z, h, lo, core):
    return ((y * NZ + z) * 2 + h, lo * 2 + core)


def along_x(h, lo, step):
    x = lax.rem(h * 2 + lo + step + 4, 4)
    return lax.div(x, 2), lax.rem(x, 2)


def plane_order(ny, nz, a, b):
    messages = {}
    for colour, n1, n2, rows, l1, l2 in (("A", nz, ny, a, "z", "y"), ("B", ny, nz, b, "y", "z")):
        for sign in (1, -1):
            for s in range(n1 - 1):
                before = (colour, sign, s - 1, -1) if s else None
                messages[colour, sign, s, -1] = (l1, sign, rows, before)
            for s in range(n1):
                for t in range(n2 - 1):
                    if t:
                        before = (colour, sign, s, t - 1)
                    else:
                        before = (colour, sign, s - 1, -1) if s else None
                    messages[colour, sign, s, t] = (l2, sign, rows, before)
    after = {}
    for key, (_, _, _, before) in messages.items():
        after.setdefault(before, []).append(key)

    def rank(key):
        return -100 if key[3] < 0 else key[3]

    free = {}
    heap = []
    count = 0

    def issue(key, now):
        nonlocal count
        axis, sign, rows, _ = messages[key]
        end = max(now, free.get((axis, sign), 0.0)) + rows * 1.024 / 46.5
        free[axis, sign] = end
        count += 1
        heapq.heappush(heap, (end + 1.8, count, key))

    first = sorted(after[None], key=rank)
    for key in first:
        issue(key, 0.0)
    events = []
    while heap:
        now, _, key = heapq.heappop(heap)
        follow = sorted(after.get(key, []), key=rank)
        for nxt in follow:
            issue(nxt, now)
        events.append((key, follow))
    return messages, first, events


def gather_kernel(
    ny, rows_a, eval_in, corpus_in, meta_in, gath, pcorpus, relay, pmeta,
    bounce, send, recv, xsend, xrecv, local_sem,
):
    nz = NZ
    rows = eval_in.shape[0]
    rows_b = rows // 2 - rows_a
    y, z, h, lo, core = place(ny)
    up_y = device(lax.rem(y + 1, ny), z, h, lo, core)
    down_y = device(lax.rem(y + ny - 1, ny), z, h, lo, core)
    up_z = device(y, lax.rem(z + 1, nz), h, lo, core)
    down_z = device(y, lax.rem(z + nz - 1, nz), h, lo, core)
    up_x = device(y, z, *along_x(h, lo, 1), core)
    down_x = device(y, z, *along_x(h, lo, -1), core)
    partner = device(y, z, 1 - h, lo, core)
    targets = {("y", 1): up_y, ("y", -1): down_y, ("z", 1): up_z, ("z", -1): down_z}

    barrier = pltpu.get_barrier_semaphore()
    peers = (up_y, down_y, up_z, down_z, up_x, down_x, partner)
    for peer in peers:
        pl.semaphore_signal(barrier, inc=1, device_id=peer, device_id_type=MESH)
    pl.semaphore_wait(barrier, len(peers))

    messages, first, events = plane_order(ny, nz, rows_a, rows_b)
    number = {key: i for i, key in enumerate(messages)}
    start_row = {("A", 1): 0, ("A", -1): rows_a, ("B", 1): 2 * rows_a, ("B", -1): 2 * rows_a + rows_b}

    def copy(key):
        colour, sign, s, t = key
        axis, _, size, before = messages[key]
        span = pl.ds(start_row[colour, sign], size)
        if t < 0:
            back1, back2 = s, 0
        else:
            back1, back2 = s, t
        if colour == "A":
            oz, oy = z - sign * back1, y - sign * back2
        else:
            oy, oz = y - sign * back1, z - sign * back2
        slot = lax.rem(oy + ny, ny) * nz + lax.rem(oz + nz, nz)
        src = eval_in.at[span] if before is None else gath.at[slot, span]
        i = number[key]
        return pltpu.make_async_remote_copy(
            src_ref=src, dst_ref=gath.at[slot, span], send_sem=send.at[i], recv_sem=recv.at[i],
            device_id=targets[axis, sign], device_id_type=MESH,
        )

    for key in first:
        copy(key).start()

    half = corpus_in.shape[0] // 2
    low, high = pl.ds(0, half), pl.ds(half, half)

    def xcopy(i, src, dst, target):
        return pltpu.make_async_remote_copy(
            src_ref=src, dst_ref=dst, send_sem=xsend.at[i], recv_sem=xrecv.at[i],
            device_id=target, device_id_type=MESH,
        )

    hop1 = [
        xcopy(0, corpus_in.at[low], relay.at[low], up_x),
        xcopy(1, corpus_in.at[high], relay.at[high], down_x),
    ]
    hop2 = [
        xcopy(2, relay.at[low], pcorpus.at[low], up_x),
        xcopy(3, relay.at[high], pcorpus.at[high], down_x),
    ]
    lists = xcopy(4, meta_in, pmeta, partner)
    lists.start()
    for c in hop1:
        c.start()
    own_slot = y * nz + z
    into = pltpu.make_async_copy(eval_in, bounce, local_sem)
    into.start()
    into.wait()
    back = pltpu.make_async_copy(bounce, gath.at[own_slot], local_sem)
    back.start()

    relay_after = len(events) // 4
    for n, (key, follow) in enumerate(events):
        if n == relay_after:
            for c, d in zip(hop1, hop2):
                c.wait_recv()
                d.start()
        copy(key).wait_recv()
        for nxt in follow:
            copy(nxt).start()
    back.wait()
    lists.wait()
    for c in hop2:
        c.wait()
    for c in hop1:
        c.wait_send()
    for key in messages:
        copy(key).wait_send()


def gather(ny, rows_a, eval_in, corpus_in, meta):
    n = len(plane_order(ny, NZ, 1, 1)[0])
    return pl.pallas_call(
        functools.partial(gather_kernel, ny, rows_a),
        name="plane_gather",
        out_shape=(
            jax.ShapeDtypeStruct((ny * NZ,) + eval_in.shape, eval_in.dtype),
            jax.ShapeDtypeStruct(corpus_in.shape, corpus_in.dtype),
            jax.ShapeDtypeStruct(corpus_in.shape, corpus_in.dtype),
            jax.ShapeDtypeStruct(meta.shape, meta.dtype),
        ),
        in_specs=[pl.BlockSpec(memory_space=pl.ANY)] * 3,
        out_specs=[pl.BlockSpec(memory_space=pl.ANY)] * 4,
        scratch_shapes=[
            pltpu.VMEM(eval_in.shape, eval_in.dtype),
            pltpu.SemaphoreType.DMA((n,)),
            pltpu.SemaphoreType.DMA((n,)),
            pltpu.SemaphoreType.DMA((5,)),
            pltpu.SemaphoreType.DMA((5,)),
            pltpu.SemaphoreType.DMA,
        ],
        compiler_params=pltpu.CompilerParams(collective_id=0, has_side_effects=True),
    )(eval_in, corpus_in, meta)


def dot_kernel(
    pairs, docs, slots, tiles_slice, meta, pmeta, lists, gath, corpus, pcorpus, part,
    evals, texts, table, codes, ring, zero, load_sem, out_sem,
):
    nb, rows, _ = gath.shape
    tile = rows // slots
    h = lax.rem(lax.axis_index("corpus"), 2)
    loads = [
        pltpu.make_async_copy(gath, evals, load_sem.at[0]),
        pltpu.make_async_copy(corpus, texts.at[0], load_sem.at[1]),
        pltpu.make_async_copy(pcorpus, texts.at[1], load_sem.at[2]),
    ]
    for c in loads:
        c.start()
    zero[...] = jnp.zeros_like(zero)

    def read(shard, i):
        return (meta, pmeta)[shard][i // 128, i % 128]

    width = lists.shape[1]
    for shard in range(2):
        for k in range(docs):
            code = jnp.zeros((1, width), jnp.int32)
            for i in range(slots):
                ids = lists[i : i + 1, :]
                hit = jnp.zeros((1, width), jnp.int32)
                for j in range(slots):
                    own = read(shard, 2 * pairs + k * slots + j)
                    hit = jnp.where(ids == own, j + 1, hit)
                code += jnp.where(ids < tiles_slice, hit, 0) * (4**i)
            table[shard * docs + k : shard * docs + k + 1, 0:width] = code
    send = pltpu.make_async_copy(table, codes, load_sem.at[3])
    send.start()
    send.wait()
    for c in loads:
        c.wait()

    depth = ring.shape[0]
    for shard in range(2):
        lists_of = (meta, pmeta)[shard]
        at = 2 * pairs + docs * slots
        count = lists_of[at // 128, at % 128]

        def one_pair(p, _, shard=shard, lists_of=lists_of, count=count):
            e = lists_of[lax.div(p, 128), lax.rem(p, 128)]
            q = p + pairs
            k = lists_of[lax.div(q, 128), lax.rem(q, 128)]
            code = codes[shard * docs + k, e]
            live = (p < count) & (lax.rem(e, 2) == h) & (code > 0)
            n = lax.rem(p, depth)

            @pl.when(jnp.logical_or(p >= depth, shard > 0))
            def _():
                pltpu.make_async_copy(ring.at[0], part.at[0, 0], out_sem.at[n]).wait()

            @pl.when(jnp.logical_not(live))
            def _():
                pltpu.make_async_copy(zero, part.at[shard, p], out_sem.at[n]).start()

            @pl.when(live)
            def _():
                ring[n] = jnp.zeros(ring.shape[1:], jnp.float32)
                block = lax.div(e, 2)
                for i in range(slots):
                    j = lax.rem(lax.div(code, 4**i), 4)

                    @pl.when(j > 0)
                    def _():
                        first = pl.multiple_of((k * slots + j - 1) * tile, tile)
                        ring[n] += lax.dot_general(
                            evals[block, pl.ds(i * tile, tile), :],
                            texts[shard, pl.ds(first, tile), :],
                            (((1,), (1,)), ((), ())),
                            preferred_element_type=jnp.float32,
                        )

                pltpu.make_async_copy(ring.at[n], part.at[shard, p], out_sem.at[n]).start()

            return 0

        lax.fori_loop(0, pairs, one_pair, 0)
    for n in range(depth):
        pltpu.make_async_copy(ring.at[0], part.at[0, 0], out_sem.at[n]).wait()


def partial_dots(pairs, docs, slots, tiles_slice, meta, pmeta, lists, gath, corpus, pcorpus):
    tile = gath.shape[1] // slots
    smem = pl.BlockSpec(memory_space=pltpu.SMEM)
    anyspace = pl.BlockSpec(memory_space=pl.ANY)
    return pl.pallas_call(
        functools.partial(dot_kernel, pairs, docs, slots, tiles_slice),
        name="partial_dots",
        out_shape=jax.ShapeDtypeStruct((2, pairs, tile, tile), jnp.float32),
        in_specs=[smem, smem, pl.BlockSpec(memory_space=pltpu.VMEM), anyspace, anyspace, anyspace],
        out_specs=anyspace,
        scratch_shapes=[
            pltpu.VMEM(gath.shape, gath.dtype),
            pltpu.VMEM((2,) + corpus.shape, corpus.dtype),
            pltpu.VMEM((8, 128), jnp.int32),
            pltpu.SMEM((8, 128), jnp.int32),
            pltpu.VMEM((8, tile, tile), jnp.float32),
            pltpu.VMEM((tile, tile), jnp.float32),
            pltpu.SemaphoreType.DMA((4,)),
            pltpu.SemaphoreType.DMA((8,)),
        ],
    )(meta, pmeta, lists, gath, corpus, pcorpus)


def reduce_kernel(
    ny, quarter, part, out, own, sib, outq, outs, inq, ins,
    lsem, dsend, drecv, qsend, qrecv, ssend, srecv,
):
    half = quarter // 2
    y, z, h, lo, core = place(ny)
    up = device(y, z, *along_x(h, lo, 1), core)
    down = device(y, z, *along_x(h, lo, -1), core)
    sibling = device(y, z, h, lo, 1 - core)
    barrier = pltpu.get_barrier_semaphore()
    for peer in (up, down, sibling):
        pl.semaphore_signal(barrier, inc=1, device_id=peer, device_id_type=MESH)
    pl.semaphore_wait(barrier, 3)

    def chunk_list(step, begin):
        return [(step % 4, begin + k, min(CHUNK, half - k)) for k in range(0, half, CHUNK)]

    groups = [
        (0, "far", chunk_list(2, 0)),
        (1, "far", chunk_list(2, half)),
        (0, "near", chunk_list(1, half)),
        (1, "near", chunk_list(-1, 0)),
        (0, "join", chunk_list(1, 0)),
        (1, "join", chunk_list(-1, half)),
        (2, "mine", chunk_list(0, 0)),
        (3, "mine", chunk_list(0, half)),
    ]
    steps = len(groups[0][2])
    order = []
    for pair in range(0, len(groups), 2):
        for s in range(steps):
            for g in (pair, pair + 1):
                order.append((g, s))
    loads = {}
    for i, (g, s) in enumerate(order):
        step, begin, size = groups[g][2][s]
        hx, lx = along_x(h, lo, step)
        shard = lax.rem(hx + h, 2)
        mine = (lx * 2 + core) * quarter + begin
        theirs = (lx * 2 + 1 - core) * quarter + begin
        span = pl.ds(begin, size)
        a = pltpu.make_async_copy(
            part.at[shard, pl.ds(mine, size)], own.at[step, span], lsem.at[i]
        )
        b = pltpu.make_async_remote_copy(
            src_ref=part.at[shard, pl.ds(theirs, size)], dst_ref=sib.at[step, span],
            send_sem=dsend.at[i], recv_sem=drecv.at[i], device_id=sibling, device_id_type=MESH,
        )
        a.start()
        b.start()
        loads[g, s] = (a, b)

    stage = {"far": 0, "near": 1, "join": 2}
    sends = []

    def message(way, kind, s):
        n = (way * 3 + stage[kind]) * steps + s
        span = pl.ds(n * CHUNK, CHUNK)
        target = up if way == 0 else down
        q = pltpu.make_async_remote_copy(
            src_ref=outq.at[span], dst_ref=inq.at[span], send_sem=qsend.at[n],
            recv_sem=qrecv.at[n], device_id=target, device_id_type=MESH,
        )
        t = pltpu.make_async_remote_copy(
            src_ref=outs.at[n], dst_ref=ins.at[n], send_sem=ssend.at[n],
            recv_sem=srecv.at[n], device_id=target, device_id_type=MESH,
        )
        return n, q, t

    def widened(n, k):
        scale = ins[n, pl.ds(k, 1), :] * (1.0 / 65534.0)
        return (inq[n * CHUNK + k].astype(jnp.int32).astype(jnp.float32) + 32767.0) * scale

    for g, s in order:
        way, kind, chunks = groups[g]
        step, begin, size = chunks[s]
        a, b = loads[g, s]
        a.wait()
        b.wait_recv()
        if kind == "mine":

            def add(k, _, step=step, begin=begin):
                own[step, begin + k] += sib[step, begin + k]
                return 0

            lax.fori_loop(0, size, add, 0)
            continue
        joined = None
        if kind == "join":
            joined, q, t = message(way, "far", s)
            q.wait_recv()
            t.wait_recv()
        n, q, t = message(way, kind, s)

        def pack(k, _, step=step, begin=begin, joined=joined, n=n):
            total = own[step, begin + k] + sib[step, begin + k]
            if joined is not None:
                total += widened(joined, k)
            top = jnp.max(total, axis=0, keepdims=True)
            outs[n, pl.ds(k, 1), :] = top
            scaled = total * (65534.0 / jnp.maximum(top, 1e-30)) - 32767.0
            outq[n * CHUNK + k] = jnp.round(scaled).astype(jnp.int32).astype(jnp.int16)
            return 0

        lax.fori_loop(0, size, pack, 0)
        q.start()
        t.start()
        sends.append((q, t))

    for kind in ("near", "join"):
        for s in range(steps):
            for way in (0, 1):
                n, q, t = message(way, kind, s)
                q.wait_recv()
                t.wait_recv()
                begin = half * ((kind == "near") ^ (way == 1)) + s * CHUNK

                def finish(k, _, begin=begin, n=n):
                    own[0, begin + k] += widened(n, k)
                    return 0

                lax.fori_loop(0, CHUNK, finish, 0)
    done = pltpu.make_async_copy(own.at[0], out, lsem.at[0])
    done.start()
    for q, t in sends:
        q.wait_send()
        t.wait_send()
    for g, s in order:
        loads[g, s][1].wait_send()
    done.wait()


def reduce(ny, part):
    pairs, tile = part.shape[1], part.shape[2]
    quarter = pairs // 4
    n = 2 * 3 * (quarter // 2 // CHUNK)
    m = 8 * (quarter // 2 // CHUNK)
    dma = pltpu.SemaphoreType.DMA
    return pl.pallas_call(
        functools.partial(reduce_kernel, ny, quarter),
        name="ring_reduce",
        out_shape=jax.ShapeDtypeStruct((quarter, tile, tile), jnp.float32),
        in_specs=[pl.BlockSpec(memory_space=pl.ANY)],
        out_specs=pl.BlockSpec(memory_space=pl.ANY),
        scratch_shapes=[
            pltpu.VMEM((4, quarter, tile, tile), jnp.float32),
            pltpu.VMEM((4, quarter, tile, tile), jnp.float32),
            pltpu.VMEM((n * CHUNK, tile, tile), jnp.int16),
            pltpu.VMEM((n, 8, tile), jnp.float32),
            pltpu.VMEM((n * CHUNK, tile, tile), jnp.int16),
            pltpu.VMEM((n, 8, tile), jnp.float32),
            dma((m,)), dma((m,)), dma((m,)), dma((n,)), dma((n,)), dma((n,)), dma((n,)),
        ],
        compiler_params=pltpu.CompilerParams(collective_id=1, has_side_effects=True),
    )(part)


def local(
    ny,
    eval_tiles,
    eval_tile_list,
    corpus_tiles,
    corpus_tile_list,
    pair_eval_block,
    pair_corpus_block,
    pair_count,
    eval_norm,
    corpus_norm,
):
    slices = lax.axis_size("vocab")
    docs, slots, tile_rows, term_width = corpus_tiles.shape
    tiles_slice = VOCAB // (term_width * slices)
    pairs = pair_eval_block.shape[0]
    quarter = pairs // slices
    rows = slots * tile_rows
    used = 2 * pairs + docs * slots + 1
    meta = jnp.concatenate(
        [
            pair_eval_block,
            pair_corpus_block,
            corpus_tile_list.reshape(-1),
            pair_count,
            jnp.zeros((-used % 1024,), jnp.int32),
        ]
    ).reshape(-1, 128)
    eval_in = eval_tiles.reshape(rows, term_width)
    corpus_in = corpus_tiles.reshape(docs * rows, term_width)
    rows_a = rows * 7 // 24
    gath, pcorpus, _, pmeta = gather(ny, rows_a, eval_in, corpus_in, meta)
    part = partial_dots(
        pairs, docs, slots, tiles_slice, meta, pmeta, eval_tile_list.T, gath, corpus_in, pcorpus
    )
    summed = reduce(ny, part)
    position = jnp.arange(pairs, dtype=jnp.int32)
    own_live = position < pair_count[0]
    first_pair = lax.axis_index("vocab") * quarter
    mine_eval = lax.dynamic_slice_in_dim(pair_eval_block, first_pair, quarter)
    mine_block = lax.dynamic_slice_in_dim(pair_corpus_block, first_pair, quarter)
    mine_live = lax.dynamic_slice_in_dim(own_live, first_pair, quarter)
    eval_scale = eval_norm.reshape(-1, tile_rows)[mine_eval]
    corpus_scale = corpus_norm.reshape(-1, tile_rows)[mine_block]
    cosine = summed / (eval_scale[:, :, None] * corpus_scale[:, None, :])
    return jnp.where(mine_live[:, None, None], cosine, 0.0)


def solution(mesh):
    ny = mesh.shape["corpus"] // (2 * NZ)
    in_specs = (
        P("corpus", "vocab", None, None),
        P(None, "vocab"),
        P("corpus", "vocab", None, None),
        P("corpus", "vocab"),
        P("corpus"),
        P("corpus"),
        P("corpus"),
        P(),
        P("corpus"),
    )
    out_specs = P(("corpus", "vocab"), None, None)
    return jax.shard_map(
        functools.partial(local, ny), mesh=mesh, in_specs=in_specs, out_specs=out_specs, check_vma=False
    )
```
